512 devices in a mesh: view: 8 (over y, x_lo), tile: 64 (over x_hi, z, core).
Axes of the slice: x: 4 (x_hi: 2, x_lo: 2; x = x_hi * 2 + x_lo), y: 4, z: 16, core: 2. Of those that a mesh axis runs over, the one named last changes fastest.
Arguments:
- estimate: float32 [128, 2048, 128], P('view', 'tile'), may hold values from 0.5 to 2
- images: float32 [8, 128, 2048, 128], P('view', None, 'tile'), may hold values from 0.2 to 2
- profiles: float32 [8, 3, 15], P('view'), may hold values from 0.02 to 0.15
Outputs:
- updated: float32 [128, 2048, 128], P('view', 'tile')
The draws below stay inside these ranges and needn't reach their ends.
All inputs are finite; a program needn't handle non-finite values.
Results may differ from the reference program's by a relative error of at most 0.0003.
Values sent between devices are 32-bit elements; how exact they have to be, the bound alone decides.
A program may use at most 64 MiB of HBM per device.

```python
import math
import jax
import jax.numpy as jnp
from jax import lax

TAPS = 15
VIEWS = 8
NY = 128
CZ = 16
NX = 2048
NZ = 128


def block_levels(key, dims, cuts, least, high):
    level, own = 1.0, jax.random.fold_in(key, 6)
    for position, shards_of in cuts:
        steps = jnp.exp(jax.random.uniform(jax.random.fold_in(own, position), (shards_of,), jnp.float32, least / len(cuts), high / len(cuts)))
        level = level * jnp.repeat(steps, dims[position] // shards_of).reshape([-1 if axis == position else 1 for axis in range(len(dims))])
    return level


def setup_inputs(seed: int = 0) -> dict:
    keys = jax.random.split(jax.random.key(seed), 4)
    estimate = jnp.clip(0.5 + 1.5 * jax.random.uniform(keys[0], (NZ, NX, NY), jnp.float32) ** block_levels(keys[0], (NZ, NX, NY), ((0, 8), (1, 64)), -0.2, 0.2), 0.5, 2.0)
    images = jnp.clip(0.2 + 1.8 * jax.random.uniform(keys[1], (VIEWS, NZ, NX, NY), jnp.float32) ** block_levels(keys[1], (VIEWS, NZ, NX, NY), ((0, 8), (2, 64)), -0.2, 0.2), 0.2, 2.0)
    profiles = jnp.clip(jnp.exp(math.log(0.15) - 2.014903 * jax.random.uniform(keys[2], (VIEWS, 3, TAPS), jnp.float32) ** block_levels(keys[2], (VIEWS, 3, TAPS), ((0, 8),), -0.2, 0.2)), 0.02, 0.15)
    return dict(estimate=estimate, images=images, profiles=profiles)


def valid_pass(padded, kernel, dimension):
    length = kernel.shape[0]
    extent = padded.shape[dimension] - length + 1
    summed = kernel[0] * lax.slice_in_dim(padded, 0, extent, axis=dimension)
    for offset in range(1, length):
        summed = summed + kernel[offset] * lax.slice_in_dim(padded, offset, offset + extent, axis=dimension)
    return summed


def correlate(volume, kernel, dimension):
    radius = kernel.shape[0] // 2
    padding = [(0, 0)] * volume.ndim
    padding[dimension] = (radius, radius)
    return valid_pass(jnp.pad(volume, padding), kernel, dimension)


def update(current, observed, kernel):
    blurred = correlate(correlate(correlate(current, kernel[0], 0), kernel[2], 2), kernel[1], 1)
    quotient = observed / blurred
    backward = correlate(quotient, kernel[1][::-1], 1)
    backward = correlate(backward, kernel[2][::-1], 2)
    backward = correlate(backward, kernel[0][::-1], 0)
    return current * backward


def reference(estimate, images, profiles):
    slabs = estimate.reshape(VIEWS, CZ, NX, NY)

    def one_slab(packed):
        current, slab_index = packed

        def advance(section_index, current):
            view_now = ((slab_index + section_index) % VIEWS).astype(jnp.int32)
            start = (slab_index * CZ).astype(jnp.int32)
            anchor = jnp.zeros((), jnp.int32)
            observed = lax.dynamic_slice(images, (view_now, start, anchor, anchor), (1, CZ, NX, NY))[0]
            kernel = lax.dynamic_index_in_dim(profiles, view_now, 0, keepdims=False)
            return update(current, observed, kernel)

        return lax.fori_loop(0, VIEWS, advance, current)

    result = lax.map(one_slab, (slabs, jnp.arange(VIEWS, dtype=jnp.int32)))
    return result.reshape(NZ, NX, NY)
```

```python
import functools

import jax
import jax.numpy as jnp
from jax import lax
from jax.experimental import pallas as pl
from jax.experimental.pallas import tpu as pltpu
from jax.sharding import PartitionSpec as P

MESH = pl.DeviceIdType.MESH
TAPS = 15
RADIUS = 7
STEP = 8
WIDE = 3 * STEP
AHEAD = 3


def split(value):
    high = value.astype(jnp.bfloat16)
    low = (value - high.astype(jnp.float32)).astype(jnp.bfloat16)
    return high, low


def dot(a, b):
    return jnp.dot(a, b, preferred_element_type=jnp.float32)


def offsets(depth, width):
    lanes = depth * WIDE
    column = lax.broadcasted_iota(jnp.int32, (depth, lanes), 1)
    plane = (column * 2731) >> 16
    dz = plane - lax.broadcasted_iota(jnp.int32, (depth, lanes), 0)
    column = lax.broadcasted_iota(jnp.int32, (STEP, lanes), 1)
    row = column - ((column * 2731) >> 16) * WIDE
    dx = row - lax.broadcasted_iota(jnp.int32, (STEP, lanes), 0) - STEP
    dy = lax.broadcasted_iota(jnp.int32, (width, width), 0) - lax.broadcasted_iota(
        jnp.int32, (width, width), 1
    )
    return dz, dx, dy


def banded(difference, taps, sign):
    result = jnp.zeros(difference.shape, jnp.float32)
    for k in range(TAPS):
        result = jnp.where(difference == sign * (k - RADIUS), taps[:, k : k + 1], result)
    return result


def matrices(profile, dz, dx, dy, sign):
    gz = banded(dz, profile[0:1], sign)
    gx = banded(dx, profile[1:2], sign)
    left = (gz[:, None, :] * gx[None, :, :]).reshape(dz.shape[0] * STEP, dz.shape[1])
    return split(left), split(banded(dy, profile[2:3], sign))


def correlate(block, left, left_high, right_high, right_low):
    depth, _, width = block.shape
    rows = depth * STEP
    flat = [block[:, i * STEP : i * STEP + WIDE, :].reshape(depth * WIDE, width) for i in (0, 1)]
    high, low = split(jnp.concatenate(flat, axis=1))
    both = dot(left, high)
    mid = both[:rows] + (both[rows:] + dot(left_high, low))
    mid = jnp.concatenate([mid[:, :width], mid[:, width:]], axis=0)
    high, low = split(mid)
    out = dot(high, right_high) + (dot(low, right_high) + dot(high, right_low))
    return [out[i * rows : (i + 1) * rows].reshape(depth, STEP, width) for i in (0, 1)]


def kernel(views, tiles, est, img, prof, out, ext, shots, quot, prof_all, zx, yy,
           load_sem, s_send, s_recv, i_send, i_recv, p_send, p_recv):
    view, tile = lax.axis_index("view"), lax.axis_index("tile")
    depth, rows, width = est.shape
    half = rows // 2
    wide = depth * STEP

    def around(value, size):
        return lax.rem(value + size, size)

    barrier = pltpu.get_barrier_semaphore()
    for dv in range(views):
        for dt in (0, 1, -1):
            if dv or dt:
                pl.semaphore_signal(
                    barrier, inc=1, device_id=(around(view + dv, views), around(tile + dt, tiles)),
                    device_id_type=MESH,
                )

    def own_image():
        return pltpu.make_async_copy(
            img.at[pl.ds(pl.multiple_of(view * depth, depth), depth)],
            shots.at[0, :, pl.ds(STEP, rows), :], load_sem.at[0])

    def own_slab():
        return pltpu.make_async_copy(est, ext.at[0, :, pl.ds(half, rows), :], load_sem.at[1])

    own_image().start()
    own_slab().start()

    def rim(n, side, first=False):
        here = pl.multiple_of(half * side, half)
        source = est.at[:, pl.ds(here, half), :] if first else ext.at[
            n, :, pl.ds(pl.multiple_of(half + half * side, half), half), :]
        return pltpu.make_async_remote_copy(
            src_ref=source,
            dst_ref=ext.at[n, :, pl.ds(pl.multiple_of((half + rows) * (1 - side), half), half), :],
            send_sem=s_send.at[n, side], recv_sem=s_recv.at[n, side],
            device_id=(view, around(tile + 2 * side - 1, tiles)), device_id_type=MESH)

    def block(n):
        to = around(view - n, views)
        return to, pl.ds(pl.multiple_of(to * depth, depth), depth)

    def shot(n):
        to, planes = block(n)
        return pltpu.make_async_remote_copy(
            src_ref=img.at[planes], dst_ref=shots.at[n, :, pl.ds(STEP, rows), :],
            send_sem=i_send.at[n, 2], recv_sem=i_recv.at[n, 2],
            device_id=(to, tile), device_id_type=MESH)

    def shot_rim(n, side):
        to, planes = block(n)
        here = pl.multiple_of((rows - STEP) * side, STEP)
        there = pl.multiple_of((rows + STEP) * (1 - side), STEP)
        return pltpu.make_async_remote_copy(
            src_ref=img.at[planes, pl.ds(here, STEP), :],
            dst_ref=shots.at[n, :, pl.ds(there, STEP), :],
            send_sem=i_send.at[n, side], recv_sem=i_recv.at[n, side],
            device_id=(to, around(tile + 2 * side - 1, tiles)), device_id_type=MESH)

    def taps(n):
        return pltpu.make_async_remote_copy(
            src_ref=prof, dst_ref=prof_all.at[n], send_sem=p_send.at[n], recv_sem=p_recv.at[n],
            device_id=(around(view - n, views), tile), device_id_type=MESH)

    def send_shots(n):
        shot(n).start()
        shot_rim(n, 0).start()
        shot_rim(n, 1).start()

    prof_all[0] = prof[...]
    dz, dx, dy = offsets(depth, width)
    pl.semaphore_wait(barrier, 3 * views - 1)

    for side in (0, 1):
        rim(0, side, True).start()
    for side in (0, 1):
        shot_rim(0, side).start()
    for n in range(1, views):
        taps(n).start()
    for n in range(1, AHEAD):
        send_shots(n)
    own_image().wait()
    own_slab().wait()

    def forward(n, start):
        got = correlate(ext[n, :, pl.ds(start, rows), :], zx[0], zx[0, :wide], yy[0, 0], yy[0, 1])
        return [shots[n, :, pl.ds(start + i * STEP, STEP), :] / got[i] for i in (0, 1)]

    odd = lax.rem(tile, 2)

    def update(n, carry):
        @pl.when(n + AHEAD < views)
        def _():
            send_shots(n + AHEAD)

        @pl.when(n > 0)
        def _():
            taps(n).wait_recv()

        profile = prof_all[n]
        for which, sign in ((0, 1), (1, -1)):
            left, right = matrices(profile, dz, dx, dy, sign)
            zx[which, :wide] = left[0]
            zx[which, wide:] = left[1]
            yy[which, 0] = right[0]
            yy[which, 1] = right[1]

        @pl.when(n > 0)
        def _():
            shot(n).wait_recv()

        inner = forward(n, half)
        for i in (0, 1):
            quot[:, half + i * STEP : half + (i + 1) * STEP, :] = inner[i]

        def one_side(number, carry):
            side = number * odd + (1 - number) * (1 - odd)
            edge = tile == side * (tiles - 1)
            start = pl.multiple_of(side * rows, rows)
            rim(n, 1 - side).wait_recv()
            shot_rim(n, 1 - side).wait_recv()

            @pl.when(edge)
            def _():
                ext[n, :, pl.ds(pl.multiple_of((half + rows) * side, half), half), :] = jnp.zeros(
                    (depth, half, width), jnp.float32)

            got = forward(n, start)
            for i in (0, 1):
                value = jnp.where(jnp.logical_and(edge, side == i), 0.0, got[i])
                quot[:, pl.ds(pl.multiple_of(start + i * STEP, STEP), STEP), :] = value
            begin = pl.multiple_of(side * half, half)
            got = correlate(quot[:, pl.ds(begin, rows), :], zx[1], zx[1, :wide], yy[1, 0], yy[1, 1])
            for i in (0, 1):
                place = pl.ds(pl.multiple_of(half + begin + i * STEP, STEP), STEP)
                ext[n + 1, :, place, :] = ext[n, :, place, :] * got[i]

            @pl.when(n < views - 1)
            def _():
                rim(n + 1, side).start()

            return carry

        return lax.fori_loop(0, 2, one_side, carry)

    lax.fori_loop(0, views, update, 0)
    out[...] = ext[views, :, pl.ds(half, rows), :]

    def drain(n, carry):
        for side in (0, 1):
            rim(n, side).wait_send()
            shot_rim(n, side).wait_send()

        @pl.when(n > 0)
        def _():
            shot(n).wait_send()
            taps(n).wait_send()

        return carry

    lax.fori_loop(0, views, drain, 0)


def shards(views, tiles, estimate, images, profiles):
    depth, rows, width = estimate.shape
    profile = jnp.pad(profiles[0], ((0, 5), (0, width - TAPS)))
    anywhere, vmem = (pl.BlockSpec(memory_space=space) for space in (pl.ANY, pltpu.VMEM))
    return pl.pallas_call(
        functools.partial(kernel, views, tiles),
        out_shape=jax.ShapeDtypeStruct(estimate.shape, estimate.dtype),
        in_specs=[anywhere, anywhere, vmem],
        out_specs=vmem,
        scratch_shapes=[
            pltpu.VMEM((views + 1, depth, 2 * rows, width), jnp.float32),
            pltpu.VMEM((views, depth, rows + 2 * STEP, width), jnp.float32),
            pltpu.VMEM((depth, rows + 2 * STEP, width), jnp.float32),
            pltpu.VMEM((views, 8, width), jnp.float32),
            pltpu.VMEM((2, 2 * depth * STEP, depth * WIDE), jnp.bfloat16),
            pltpu.VMEM((2, 2, width, width), jnp.bfloat16),
            pltpu.SemaphoreType.DMA((2,)),
            pltpu.SemaphoreType.DMA((views, 2)),
            pltpu.SemaphoreType.DMA((views, 2)),
            pltpu.SemaphoreType.DMA((views, 3)),
            pltpu.SemaphoreType.DMA((views, 3)),
            pltpu.SemaphoreType.DMA((views,)),
            pltpu.SemaphoreType.DMA((views,)),
        ],
        compiler_params=pltpu.CompilerParams(
            collective_id=0, has_side_effects=True, vmem_limit_bytes=48 << 20),
    )(estimate, images[0], profile)


def solution(mesh):
    return jax.shard_map(
        functools.partial(shards, mesh.shape["view"], mesh.shape["tile"]),
        mesh=mesh,
        in_specs=(P("view", "tile", None), P("view", None, "tile", None), P("view", None, None)),
        out_specs=P("view", "tile", None),
        check_vma=False,
    )
```

```python
import functools

import jax
import jax.numpy as jnp
from jax import lax
from jax.experimental import pallas as pl
from jax.experimental.pallas import tpu as pltpu
from jax.sharding import PartitionSpec as P

MESH = pl.DeviceIdType.MESH
TAPS = 15
RADIUS = 7
STEP = 8
WIDE = 3 * STEP
AHEAD = 3


def split(value):
    high = value.astype(jnp.bfloat16)
    low = (value - high.astype(jnp.float32)).astype(jnp.bfloat16)
    return high, low


def dot(a, b):
    return jnp.dot(a, b, preferred_element_type=jnp.float32)


def offsets(depth, width):
    lanes = depth * WIDE
    column = lax.broadcasted_iota(jnp.int32, (depth, lanes), 1)
    plane = (column * 2731) >> 16
    dz = plane - lax.broadcasted_iota(jnp.int32, (depth, lanes), 0)
    column = lax.broadcasted_iota(jnp.int32, (STEP, lanes), 1)
    row = column - ((column * 2731) >> 16) * WIDE
    dx = row - lax.broadcasted_iota(jnp.int32, (STEP, lanes), 0) - STEP
    dy = lax.broadcasted_iota(jnp.int32, (width, width), 0) - lax.broadcasted_iota(
        jnp.int32, (width, width), 1
    )
    return dz, dx, dy


def banded(difference, taps, sign):
    result = jnp.zeros(difference.shape, jnp.float32)
    for k in range(TAPS):
        result = jnp.where(difference == sign * (k - RADIUS), taps[:, k : k + 1], result)
    return result


def matrices(profile, dz, dx, dy, sign):
    gz = banded(dz, profile[0], sign)
    gx = banded(dx, profile[1], sign)
    left = (gz[:, None, :] * gx[None, :, :]).reshape(dz.shape[0] * STEP, dz.shape[1])
    return split(left), split(banded(dy, profile[2], sign))


def correlate(block, left, left_high, right_high, right_low):
    depth, _, width = block.shape
    rows = depth * STEP
    flat = [block[:, i * STEP : i * STEP + WIDE, :].reshape(depth * WIDE, width) for i in (0, 1)]
    high, low = split(jnp.concatenate(flat, axis=1))
    both = dot(left, high)
    mid = both[:rows] + (both[rows:] + dot(left_high, low))
    mid = jnp.concatenate([mid[:, :width], mid[:, width:]], axis=0)
    high, low = split(mid)
    out = dot(high, right_high) + (dot(low, right_high) + dot(high, right_low))
    return [out[i * rows : (i + 1) * rows].reshape(depth, STEP, width) for i in (0, 1)]


def kernel(views, tiles, est, img, prof, out, ext, shots, quot, prof_all, zx, yy,
           load_sem, s_send, s_recv, i_send, i_recv, p_send, p_recv):
    view, tile = lax.axis_index("view"), lax.axis_index("tile")
    depth, rows, width = est.shape
    half = rows // 2
    wide = depth * STEP

    def around(value, size):
        return lax.rem(value + size, size)

    barrier = pltpu.get_barrier_semaphore()
    for side in (0, 1):
        @pl.when(tile != side * (tiles - 1))
        def _(side=side):
            pl.semaphore_signal(
                barrier, inc=1, device_id=(view, tile + 2 * side - 1), device_id_type=MESH)

    for dv in range(1, views):
        pl.semaphore_signal(
            barrier, inc=1, device_id=(around(view + dv, views), tile), device_id_type=MESH)

    def own_image():
        return pltpu.make_async_copy(
            img.at[pl.ds(pl.multiple_of(view * depth, depth), depth)],
            shots.at[0, :, pl.ds(STEP, rows), :], load_sem.at[0])

    def own_slab():
        return pltpu.make_async_copy(est, ext.at[0, :, pl.ds(half, rows), :], load_sem.at[1])

    def own_taps():
        return pltpu.make_async_copy(prof, prof_all.at[0], load_sem.at[2])

    own_taps().start()
    own_slab().start()
    own_image().start()

    def rim(n, side, first=False):
        here = pl.multiple_of(half * side, half)
        source = est.at[:, pl.ds(here, half), :] if first else ext.at[
            n, :, pl.ds(pl.multiple_of(half + half * side, half), half), :]
        return pltpu.make_async_remote_copy(
            src_ref=source,
            dst_ref=ext.at[n, :, pl.ds(pl.multiple_of((half + rows) * (1 - side), half), half), :],
            send_sem=s_send.at[n, side], recv_sem=s_recv.at[n, side],
            device_id=(view, tile + 2 * side - 1), device_id_type=MESH)

    def block(n):
        to = around(view - n, views)
        return to, pl.ds(pl.multiple_of(to * depth, depth), depth)

    def shot(n):
        to, planes = block(n)
        return pltpu.make_async_remote_copy(
            src_ref=img.at[planes], dst_ref=shots.at[n, :, pl.ds(STEP, rows), :],
            send_sem=i_send.at[n, 2], recv_sem=i_recv.at[n, 2],
            device_id=(to, tile), device_id_type=MESH)

    def shot_rim(n, side, first=False):
        here = (rows - STEP) * side
        there = pl.multiple_of((rows + STEP) * (1 - side), STEP)
        source = img.at[block(0)[1], pl.ds(pl.multiple_of(here, STEP), STEP), :] if first else shots.at[
            n, :, pl.ds(pl.multiple_of(STEP + here, STEP), STEP), :]
        return pltpu.make_async_remote_copy(
            src_ref=source,
            dst_ref=shots.at[n, :, pl.ds(there, STEP), :],
            send_sem=i_send.at[n, side], recv_sem=i_recv.at[n, side],
            device_id=(view, tile + 2 * side - 1), device_id_type=MESH)

    def taps(n):
        return pltpu.make_async_remote_copy(
            src_ref=prof, dst_ref=prof_all.at[n], send_sem=p_send.at[n], recv_sem=p_recv.at[n],
            device_id=(around(view - n, views), tile), device_id_type=MESH)

    dz, dx, dy = offsets(depth, width)
    at_end = (tile == 0).astype(jnp.int32) + (tile == tiles - 1).astype(jnp.int32)
    pl.semaphore_wait(barrier, views + 1 - at_end)

    for side in (0, 1):
        @pl.when(tile != side * (tiles - 1))
        def _(side=side):
            rim(0, side, True).start()
            shot_rim(0, side, True).start()

    for n in range(1, views):
        taps(n).start()
    for n in range(1, AHEAD):
        shot(n).start()
    own_taps().wait()
    own_slab().wait()
    own_image().wait()

    def forward(n, start):
        got = correlate(ext[n, :, pl.ds(start, rows), :], zx[0], zx[0, :wide], yy[0, 0], yy[0, 1])
        return [shots[n, :, pl.ds(start + i * STEP, STEP), :] / got[i] for i in (0, 1)]

    odd = lax.rem(tile, 2)

    def update(n, carry):
        @pl.when(n + AHEAD < views)
        def _():
            shot(n + AHEAD).start()

        @pl.when(n > 0)
        def _():
            taps(n).wait_recv()

        profile = prof_all[n]
        for which, sign in ((0, 1), (1, -1)):
            left, right = matrices(profile, dz, dx, dy, sign)
            zx[which, :wide] = left[0]
            zx[which, wide:] = left[1]
            yy[which, 0] = right[0]
            yy[which, 1] = right[1]

        inner = forward(n, half)
        for i in (0, 1):
            quot[:, half + i * STEP : half + (i + 1) * STEP, :] = inner[i]

        def one_side(number, carry):
            side = number * odd + (1 - number) * (1 - odd)
            edge = tile == side * (tiles - 1)
            start = pl.multiple_of(side * rows, rows)

            @pl.when(jnp.logical_and(number == 1, n < views - 1))
            def _():
                shot(n + 1).wait_recv()
                for other in (0, 1):
                    @pl.when(tile != other * (tiles - 1))
                    def _(other=other):
                        shot_rim(n + 1, other).start()

            @pl.when(jnp.logical_not(edge))
            def _():
                rim(n, 1 - side).wait_recv()
                shot_rim(n, 1 - side).wait_recv()

            @pl.when(edge)
            def _():
                ext[n, :, pl.ds(pl.multiple_of((half + rows) * side, half), half), :] = jnp.zeros(
                    (depth, half, width), jnp.float32)

            got = forward(n, start)
            for i in (0, 1):
                value = jnp.where(jnp.logical_and(edge, side == i), 0.0, got[i])
                quot[:, pl.ds(pl.multiple_of(start + i * STEP, STEP), STEP), :] = value
            begin = pl.multiple_of(side * half, half)
            got = correlate(quot[:, pl.ds(begin, rows), :], zx[1], zx[1, :wide], yy[1, 0], yy[1, 1])
            for i in (0, 1):
                place = pl.ds(pl.multiple_of(half + begin + i * STEP, STEP), STEP)
                ext[n + 1, :, place, :] = ext[n, :, place, :] * got[i]

            @pl.when(jnp.logical_and(n < views - 1, jnp.logical_not(edge)))
            def _():
                rim(n + 1, side).start()

            return carry

        return lax.fori_loop(0, 2, one_side, carry)

    lax.fori_loop(0, views, update, 0)
    out[...] = ext[views, :, pl.ds(half, rows), :]

    def drain(n, carry):
        for side in (0, 1):
            @pl.when(tile != side * (tiles - 1))
            def _(side=side):
                rim(n, side).wait_send()
                shot_rim(n, side).wait_send()

        @pl.when(n > 0)
        def _():
            shot(n).wait_send()
            taps(n).wait_send()

        return carry

    lax.fori_loop(0, views, drain, 0)


def shards(views, tiles, estimate, images, profiles):
    depth, rows, width = estimate.shape
    far, near = (pl.BlockSpec(memory_space=space) for space in (pltpu.HBM, pltpu.VMEM))
    return pl.pallas_call(
        functools.partial(kernel, views, tiles),
        out_shape=jax.ShapeDtypeStruct(estimate.shape, estimate.dtype),
        in_specs=[far, far, far],
        out_specs=near,
        scratch_shapes=[
            pltpu.VMEM((views + 1, depth, 2 * rows, width), jnp.float32),
            pltpu.VMEM((views, depth, rows + 2 * STEP, width), jnp.float32),
            pltpu.VMEM((depth, rows + 2 * STEP, width), jnp.float32),
            pltpu.VMEM((views, 3, 1, TAPS), jnp.float32),
            pltpu.VMEM((2, 2 * depth * STEP, depth * WIDE), jnp.bfloat16),
            pltpu.VMEM((2, 2, width, width), jnp.bfloat16),
            pltpu.SemaphoreType.DMA((3,)),
            pltpu.SemaphoreType.DMA((views, 2)),
            pltpu.SemaphoreType.DMA((views, 2)),
            pltpu.SemaphoreType.DMA((views, 3)),
            pltpu.SemaphoreType.DMA((views, 3)),
            pltpu.SemaphoreType.DMA((views,)),
            pltpu.SemaphoreType.DMA((views,)),
        ],
        compiler_params=pltpu.CompilerParams(
            collective_id=0, has_side_effects=True, vmem_limit_bytes=64000000),
    )(estimate, images[0], jnp.transpose(profiles, (1, 0, 2)))


def solution(mesh):
    return jax.shard_map(
        functools.partial(shards, mesh.shape["view"], mesh.shape["tile"]),
        mesh=mesh,
        in_specs=(P("view", "tile", None), P("view", None, "tile", None), P("view", None, None)),
        out_specs=P("view", "tile", None),
        check_vma=False,
    )
```

```python
import functools

import jax
import jax.numpy as jnp
from jax import lax
from jax.experimental import pallas as pl
from jax.experimental.pallas import tpu as pltpu
from jax.sharding import PartitionSpec as P

MESH = pl.DeviceIdType.MESH
TAPS = 15
RADIUS = 7
STEP = 8
WIDE = 3 * STEP
AHEAD = 4


def split(value):
    high = value.astype(jnp.bfloat16)
    low = (value - high.astype(jnp.float32)).astype(jnp.bfloat16)
    return high, low


def dot(a, b):
    return jnp.dot(a, b, preferred_element_type=jnp.float32)


def offsets(depth, width):
    lanes = depth * WIDE
    column = lax.broadcasted_iota(jnp.int32, (depth, lanes), 1)
    plane = (column * 2731) >> 16
    dz = plane - lax.broadcasted_iota(jnp.int32, (depth, lanes), 0)
    column = lax.broadcasted_iota(jnp.int32, (STEP, lanes), 1)
    row = column - ((column * 2731) >> 16) * WIDE
    dx = row - lax.broadcasted_iota(jnp.int32, (STEP, lanes), 0) - STEP
    dy = lax.broadcasted_iota(jnp.int32, (width, width), 0) - lax.broadcasted_iota(
        jnp.int32, (width, width), 1
    )
    return dz, dx, dy


def banded(difference, taps, sign):
    result = jnp.zeros(difference.shape, jnp.float32)
    for k in range(TAPS):
        result = jnp.where(difference == sign * (k - RADIUS), taps[:, k : k + 1], result)
    return result


def matrices(profile, dz, dx, dy, sign):
    gz = banded(dz, profile[0], sign)
    gx = banded(dx, profile[1], sign)
    left = (gz[:, None, :] * gx[None, :, :]).reshape(dz.shape[0] * STEP, dz.shape[1])
    return split(left), split(banded(dy, profile[2], sign))


def correlate(block, left, left_high, right_high, right_low):
    depth, _, width = block.shape
    rows = depth * STEP
    flat = [block[:, i * STEP : i * STEP + WIDE, :].reshape(depth * WIDE, width) for i in (0, 1)]
    high, low = split(jnp.concatenate(flat, axis=1))
    both = dot(left, high)
    mid = both[:rows] + (both[rows:] + dot(left_high, low))
    mid = jnp.concatenate([mid[:, :width], mid[:, width:]], axis=0)
    high, low = split(mid)
    out = dot(high, right_high) + (dot(low, right_high) + dot(high, right_low))
    return [out[i * rows : (i + 1) * rows].reshape(depth, STEP, width) for i in (0, 1)]


def kernel(views, tiles, est, img, prof, out, ext, shots, quot, middle, prof_all, zx, yy,
           load_sem, s_send, s_recv, i_send, i_recv, p_send, p_recv):
    view, tile = lax.axis_index("view"), lax.axis_index("tile")
    depth, rows, width = est.shape
    half = rows // 2
    wide = depth * STEP
    skirt = 3 * STEP

    def around(value, size):
        return lax.rem(value + size, size)

    def inside(side):
        return tile != side * (tiles - 1)

    def at(row, size=STEP):
        return pl.ds(pl.multiple_of(row, STEP), size)

    barrier = pltpu.get_barrier_semaphore()
    for side in (0, 1):
        @pl.when(inside(side))
        def _(side=side):
            pl.semaphore_signal(
                barrier, inc=1, device_id=(view, tile + 2 * side - 1), device_id_type=MESH)

    for dv in range(1, views):
        pl.semaphore_signal(
            barrier, inc=1, device_id=(around(view + dv, views), tile), device_id_type=MESH)

    def block(n):
        to = around(view - n, views)
        return to, pl.ds(pl.multiple_of(to * depth, depth), depth)

    own = [
        pltpu.make_async_copy(prof, prof_all.at[0], load_sem.at[0]),
        pltpu.make_async_copy(est, ext.at[0, :, pl.ds(rows, rows), :], load_sem.at[1]),
        pltpu.make_async_copy(
            img.at[block(0)[1]], shots.at[0, :, pl.ds(skirt, rows), :], load_sem.at[2]),
    ]
    for copy in own:
        copy.start()

    def rim(m, side, part, first=False):
        here = pl.ds(half * part, half)
        source = est.at[:, here, :] if first else ext.at[m, :, pl.ds(rows + half * part, half), :]
        return pltpu.make_async_remote_copy(
            src_ref=source,
            dst_ref=ext.at[m, :, at(2 * rows * (1 - side) + half * part, half), :],
            send_sem=s_send.at[m, side, part], recv_sem=s_recv.at[m, side, part],
            device_id=(view, tile + 2 * side - 1), device_id_type=MESH)

    def shot(n):
        to, planes = block(n)
        return pltpu.make_async_remote_copy(
            src_ref=img.at[planes], dst_ref=shots.at[n, :, pl.ds(skirt, rows), :],
            send_sem=i_send.at[n, 2], recv_sem=i_recv.at[n, 2],
            device_id=(to, tile), device_id_type=MESH)

    def shot_rim(m, second, side, first=False):
        n = 2 * m + second
        size = STEP if second else skirt
        here = (rows - size) * side
        there = (skirt + rows) * (1 - side) + (skirt - size) * side
        source = img.at[block(0)[1], at(here, size), :] if first else shots.at[
            n, :, at(skirt + here, size), :]
        return pltpu.make_async_remote_copy(
            src_ref=source, dst_ref=shots.at[n, :, at(there, size), :],
            send_sem=i_send.at[n, side], recv_sem=i_recv.at[n, side],
            device_id=(view, tile + 2 * side - 1), device_id_type=MESH)

    def taps(n):
        return pltpu.make_async_remote_copy(
            src_ref=prof, dst_ref=prof_all.at[n], send_sem=p_send.at[n], recv_sem=p_recv.at[n],
            device_id=(around(view - n, views), tile), device_id_type=MESH)

    def pass_on(m, second):
        shot(2 * m + second).wait_recv()
        for side in (0, 1):
            @pl.when(inside(side))
            def _(side=side):
                shot_rim(m, second, side).start()

    dz, dx, dy = offsets(depth, width)
    at_end = (tile == 0).astype(jnp.int32) + (tile == tiles - 1).astype(jnp.int32)
    pl.semaphore_wait(barrier, views + 1 - at_end)

    for side in (0, 1):
        @pl.when(inside(side))
        def _(side=side):
            for part in (1 - side, side):
                rim(0, side, part, True).start()
            shot_rim(0, 0, side, True).start()

    for n in range(1, views):
        taps(n).start()
    for n in range(1, AHEAD):
        shot(n).start()
    for copy in own:
        copy.wait()

    def product(window, second, back):
        return correlate(window, zx[second, back], zx[second, back, :wide],
                         yy[second, back, 0], yy[second, back, 1])

    def quotient(m, second, i, edge):
        if second:
            got = product(middle[:, at(STEP * (i + 1), rows), :], 1, 0)
        else:
            got = product(ext[m, :, at(STEP * (i + 3), rows), :], 0, 0)
        for k in (0, 1):
            value = shots[2 * m + second, :, at(STEP * (i + k) + skirt), :] / got[k]
            if edge is not None:
                beyond = jnp.logical_or(i + k < 0, i + k >= rows // STEP)
                value = jnp.where(jnp.logical_and(edge, beyond), 0.0, value)
            got[k] = value
        return got

    def keep(second, i, values):
        for k in (0, 1):
            quot[second, :, at(STEP * (i + k + (1 if second else 3))), :] = values[k]

    def pair(m, carry):
        @pl.when(2 * m + AHEAD < views)
        def _():
            shot(2 * m + AHEAD).start()

        @pl.when(2 * m + AHEAD + 1 < views)
        def _():
            shot(2 * m + AHEAD + 1).start()

        for second in (0, 1):
            n = 2 * m + second
            if second:
                taps(n).wait_recv()
            else:
                @pl.when(m > 0)
                def _():
                    taps(n).wait_recv()
            for which, sign in ((0, 1), (1, -1)):
                left, right = matrices(prof_all[n], dz, dx, dy, sign)
                zx[second, which, :wide] = left[0]
                zx[second, which, wide:] = left[1]
                yy[second, which, 0] = right[0]
                yy[second, which, 1] = right[1]

        @pl.when(m > 0)
        def _():
            pass_on(m, 0)

        keep(0, 1, quotient(m, 0, 1, None))
        pass_on(m, 1)

        def one_side(number, carry):
            odd = lax.rem(tile, 2)
            side = number * odd + (1 - number) * (1 - odd)
            edge = tile == side * (tiles - 1)

            @pl.when(jnp.logical_not(edge))
            def _():
                for part in (0, 1):
                    rim(m, 1 - side, part).wait_recv()
                shot_rim(m, 0, 1 - side).wait_recv()

            @pl.when(edge)
            def _():
                ext[m, :, at(2 * rows * side, rows), :] = jnp.zeros((depth, rows, width), jnp.float32)

            starts = [6 * side - 3, 6 * side - 1]
            for i, values in zip(starts, [quotient(m, 0, i, edge) for i in starts]):
                keep(0, i, values)

            starts = [4 * side - 2, 4 * side]
            found = [product(quot[0, :, at(STEP * (i + 2), rows), :], 0, 1) for i in starts]
            for i, got in zip(starts, found):
                for k in (0, 1):
                    middle[:, at(STEP * (i + k + 2)), :] = (
                        ext[m, :, at(STEP * (i + k + 4)), :] * got[k])

            @pl.when(jnp.logical_not(edge))
            def _():
                shot_rim(m, 1, 1 - side).wait_recv()

            keep(1, 4 * side - 1, quotient(m, 1, 4 * side - 1, edge))
            return carry

        lax.fori_loop(0, 2, one_side, 0)
        keep(1, 1, quotient(m, 1, 1, None))
        found = [product(quot[1, :, pl.ds(half * part, rows), :], 1, 1) for part in (0, 1)]
        for part in (0, 1):
            got = found[part]
            for k in (0, 1):
                ext[m + 1, :, pl.ds(rows + half * part + STEP * k, STEP), :] = (
                    middle[:, pl.ds(half + half * part + STEP * k, STEP), :] * got[k])
            for side in (0, 1):
                @pl.when(jnp.logical_and(m < views // 2 - 1, inside(side)))
                def _(side=side, part=part):
                    rim(m + 1, side, part).start()
        return carry

    lax.fori_loop(0, views // 2, pair, 0)
    result = pltpu.make_async_copy(ext.at[views // 2, :, pl.ds(rows, rows), :], out, load_sem.at[1])
    result.start()

    def drain(m, carry):
        for side in (0, 1):
            @pl.when(inside(side))
            def _(side=side):
                for k in (0, 1):
                    rim(m, side, k).wait_send()
                    shot_rim(m, k, side).wait_send()

        for second in (0, 1):
            @pl.when(2 * m + second > 0)
            def _(second=second):
                shot(2 * m + second).wait_send()
                taps(2 * m + second).wait_send()

        return carry

    lax.fori_loop(0, views // 2, drain, 0)
    result.wait()


def shards(views, tiles, estimate, images, profiles):
    depth, rows, width = estimate.shape
    far = pl.BlockSpec(memory_space=pltpu.HBM)
    return pl.pallas_call(
        functools.partial(kernel, views, tiles),
        out_shape=jax.ShapeDtypeStruct(estimate.shape, estimate.dtype),
        in_specs=[far, far, far],
        out_specs=far,
        scratch_shapes=[
            pltpu.VMEM((views // 2 + 1, depth, 3 * rows, width), jnp.float32),
            pltpu.VMEM((views, depth, rows + 6 * STEP, width), jnp.float32),
            pltpu.VMEM((2, depth, rows + 6 * STEP, width), jnp.float32),
            pltpu.VMEM((depth, rows + 4 * STEP, width), jnp.float32),
            pltpu.VMEM((views, 3, 1, TAPS), jnp.float32),
            pltpu.VMEM((2, 2, 2 * depth * STEP, depth * WIDE), jnp.bfloat16),
            pltpu.VMEM((2, 2, 2, width, width), jnp.bfloat16),
            pltpu.SemaphoreType.DMA((3,)),
            pltpu.SemaphoreType.DMA((views // 2, 2, 2)),
            pltpu.SemaphoreType.DMA((views // 2, 2, 2)),
            pltpu.SemaphoreType.DMA((views, 3)),
            pltpu.SemaphoreType.DMA((views, 3)),
            pltpu.SemaphoreType.DMA((views,)),
            pltpu.SemaphoreType.DMA((views,)),
        ],
        compiler_params=pltpu.CompilerParams(
            collective_id=0, has_side_effects=True, vmem_limit_bytes=64000000),
    )(estimate, images[0], jnp.transpose(profiles, (1, 0, 2)))


def solution(mesh):
    return jax.shard_map(
        functools.partial(shards, mesh.shape["view"], mesh.shape["tile"]),
        mesh=mesh,
        in_specs=(P("view", "tile", None), P("view", None, "tile", None), P("view", None, None)),
        out_specs=P("view", "tile", None),
        check_vma=False,
    )
```

```python
import functools

import jax
import jax.numpy as jnp
from jax import lax
from jax.experimental import pallas as pl
from jax.experimental.pallas import tpu as pltpu
from jax.sharding import PartitionSpec as P

MESH = pl.DeviceIdType.MESH
TAPS = 15
RADIUS = 7
STEP = 8
WIDE = 3 * STEP
AHEAD = 4


def split(value):
    high = value.astype(jnp.bfloat16)
    low = (value - high.astype(jnp.float32)).astype(jnp.bfloat16)
    return high, low


def dot(a, b):
    return jnp.dot(a, b, preferred_element_type=jnp.float32)


def offsets(depth, width):
    lanes = depth * WIDE
    column = lax.broadcasted_iota(jnp.int32, (depth, lanes), 1)
    plane = (column * 2731) >> 16
    dz = plane - lax.broadcasted_iota(jnp.int32, (depth, lanes), 0)
    column = lax.broadcasted_iota(jnp.int32, (STEP, lanes), 1)
    row = column - ((column * 2731) >> 16) * WIDE
    dx = row - lax.broadcasted_iota(jnp.int32, (STEP, lanes), 0) - STEP
    dy = lax.broadcasted_iota(jnp.int32, (width, width), 0) - lax.broadcasted_iota(
        jnp.int32, (width, width), 1
    )
    return dz, dx, dy


def banded(difference, taps, sign):
    result = jnp.zeros(difference.shape, jnp.float32)
    for k in range(TAPS):
        result = jnp.where(difference == sign * (k - RADIUS), taps[:, k : k + 1], result)
    return result


def matrices(profile, dz, dx, dy, sign):
    gz = banded(dz, profile[0], sign)
    gx = banded(dx, profile[1], sign)
    left = (gz[:, None, :] * gx[None, :, :]).reshape(dz.shape[0] * STEP, dz.shape[1])
    return split(left), split(banded(dy, profile[2], sign))


def correlate(block, left, left_high, right_high, right_low):
    depth, _, width = block.shape
    rows = depth * STEP
    flat = [block[:, i * STEP : i * STEP + WIDE, :].reshape(depth * WIDE, width) for i in (0, 1)]
    high, low = split(jnp.concatenate(flat, axis=1))
    both = dot(left, high)
    mid = both[:rows] + (both[rows:] + dot(left_high, low))
    mid = jnp.concatenate([mid[:, :width], mid[:, width:]], axis=0)
    high, low = split(mid)
    out = dot(high, right_high) + (dot(low, right_high) + dot(high, right_low))
    return [out[i * rows : (i + 1) * rows].reshape(depth, STEP, width) for i in (0, 1)]


def kernel(views, tiles, est, img, prof, out, ext, shots, quot, middle, prof_all, zx, yy,
           load_sem, s_send, s_recv, i_send, i_recv, p_send, p_recv):
    view, tile = lax.axis_index("view"), lax.axis_index("tile")
    depth, rows, width = est.shape
    half = rows // 2
    wide = depth * STEP
    skirt = 3 * STEP

    def around(value, size):
        return lax.rem(value + size, size)

    def inside(side):
        return tile != side * (tiles - 1)

    def at(row, size=STEP):
        return pl.ds(pl.multiple_of(row, STEP), size)

    barrier = pltpu.get_barrier_semaphore()
    for side in (0, 1):
        @pl.when(inside(side))
        def _(side=side):
            pl.semaphore_signal(
                barrier, inc=1, device_id=(view, tile + 2 * side - 1), device_id_type=MESH)

    for dv in range(1, views):
        pl.semaphore_signal(
            barrier, inc=1, device_id=(around(view + dv, views), tile), device_id_type=MESH)

    def block(n):
        to = around(view - n, views)
        return to, pl.ds(pl.multiple_of(to * depth, depth), depth)

    own = [
        pltpu.make_async_copy(prof, prof_all.at[0], load_sem.at[0]),
        pltpu.make_async_copy(est, ext.at[0, :, pl.ds(rows, rows), :], load_sem.at[1]),
        pltpu.make_async_copy(
            img.at[block(0)[1]], shots.at[0, :, pl.ds(skirt, rows), :], load_sem.at[2]),
    ]
    for copy in own:
        copy.start()

    def rim(m, side, part, first=False):
        source = est.at[:, at(half * part, half), :] if first else ext.at[
            m, :, at(rows + half * part, half), :]
        return pltpu.make_async_remote_copy(
            src_ref=source,
            dst_ref=ext.at[m, :, at(2 * rows * (1 - side) + half * part, half), :],
            send_sem=s_send.at[m, side, part], recv_sem=s_recv.at[m, side, part],
            device_id=(view, tile + 2 * side - 1), device_id_type=MESH)

    def shot(n):
        to, planes = block(n)
        return pltpu.make_async_remote_copy(
            src_ref=img.at[planes], dst_ref=shots.at[n, :, pl.ds(skirt, rows), :],
            send_sem=i_send.at[n, 2], recv_sem=i_recv.at[n, 2],
            device_id=(to, tile), device_id_type=MESH)

    def shot_rim(m, second, side, first=False):
        n = 2 * m + second
        size = STEP if second else skirt
        here = (rows - size) * side
        there = (skirt + rows) * (1 - side) + (skirt - size) * side
        source = img.at[block(0)[1], at(here, size), :] if first else shots.at[
            n, :, at(skirt + here, size), :]
        return pltpu.make_async_remote_copy(
            src_ref=source, dst_ref=shots.at[n, :, at(there, size), :],
            send_sem=i_send.at[n, side], recv_sem=i_recv.at[n, side],
            device_id=(view, tile + 2 * side - 1), device_id_type=MESH)

    def taps(n):
        return pltpu.make_async_remote_copy(
            src_ref=prof, dst_ref=prof_all.at[n], send_sem=p_send.at[n], recv_sem=p_recv.at[n],
            device_id=(around(view - n, views), tile), device_id_type=MESH)

    def pass_on(m, second):
        shot(2 * m + second).wait_recv()
        for side in (0, 1):
            @pl.when(inside(side))
            def _(side=side):
                shot_rim(m, second, side).start()

    dz, dx, dy = offsets(depth, width)
    at_end = (tile == 0).astype(jnp.int32) + (tile == tiles - 1).astype(jnp.int32)
    pl.semaphore_wait(barrier, views + 1 - at_end)

    for side in (0, 1):
        @pl.when(inside(side))
        def _(side=side):
            for part in (side, 1 - side):
                rim(0, side, part, True).start()
            shot_rim(0, 0, side, True).start()

    for n in range(1, views):
        taps(n).start()
    for n in range(1, AHEAD):
        shot(n).start()
    for copy in own:
        copy.wait()

    odd = lax.rem(tile, 2)

    def product(window, second, back):
        return correlate(window, zx[second, back], zx[second, back, :wide],
                         yy[second, back, 0], yy[second, back, 1])

    def blurred(m, second, i):
        if second:
            return product(middle[:, at(STEP * (i + 1), rows), :], 1, 0)
        return product(ext[m, :, at(STEP * (i + 3), rows), :], 0, 0)

    def keep(m, second, i, edge, got):
        for k in (0, 1):
            value = shots[2 * m + second, :, at(STEP * (i + k) + skirt), :] / got[k]
            if edge is not None:
                beyond = jnp.logical_or(i + k < 0, i + k >= rows // STEP)
                value = jnp.where(jnp.logical_and(edge, beyond), 0.0, value)
            quot[second, :, at(STEP * (i + k + (1 if second else 3))), :] = value

    def pair(m, carry):
        @pl.when(2 * m + AHEAD < views)
        def _():
            shot(2 * m + AHEAD).start()

        @pl.when(2 * m + AHEAD + 1 < views)
        def _():
            shot(2 * m + AHEAD + 1).start()

        for second in (0, 1):
            n = 2 * m + second
            if second:
                taps(n).wait_recv()
            else:
                @pl.when(m > 0)
                def _():
                    taps(n).wait_recv()
            for which, sign in ((0, 1), (1, -1)):
                left, right = matrices(prof_all[n], dz, dx, dy, sign)
                zx[second, which, :wide] = left[0]
                zx[second, which, wide:] = left[1]
                yy[second, which, 0] = right[0]
                yy[second, which, 1] = right[1]

        @pl.when(m > 0)
        def _():
            pass_on(m, 0)

        keep(m, 0, 1, None, blurred(m, 0, 1))
        pass_on(m, 1)

        def one_side(number, carry):
            side = number * odd + (1 - number) * (1 - odd)
            edge = tile == side * (tiles - 1)

            @pl.when(edge)
            def _():
                ext[m, :, at(2 * rows * side, rows), :] = jnp.zeros((depth, rows, width), jnp.float32)

            @pl.when(jnp.logical_not(edge))
            def _():
                rim(m, 1 - side, 1 - side).wait_recv()

            close = blurred(m, 0, 4 * side - 1)

            @pl.when(jnp.logical_not(edge))
            def _():
                rim(m, 1 - side, side).wait_recv()

            beyond = blurred(m, 0, 8 * side - 3)

            @pl.when(jnp.logical_not(edge))
            def _():
                shot_rim(m, 0, 1 - side).wait_recv()

            keep(m, 0, 4 * side - 1, edge, close)
            keep(m, 0, 8 * side - 3, edge, beyond)

            starts = [4 * side - 2, 4 * side]
            found = [product(quot[0, :, at(STEP * (i + 2), rows), :], 0, 1) for i in starts]
            for i, got in zip(starts, found):
                for k in (0, 1):
                    middle[:, at(STEP * (i + k + 2)), :] = (
                        ext[m, :, at(STEP * (i + k + 4)), :] * got[k])

            @pl.when(jnp.logical_not(edge))
            def _():
                shot_rim(m, 1, 1 - side).wait_recv()

            keep(m, 1, 4 * side - 1, edge, blurred(m, 1, 4 * side - 1))
            return carry

        lax.fori_loop(0, 2, one_side, 0)
        keep(m, 1, 1, None, blurred(m, 1, 1))
        for part in (odd, 1 - odd):
            got = product(quot[1, :, at(half * part, rows), :], 1, 1)
            for k in (0, 1):
                ext[m + 1, :, at(rows + half * part + STEP * k), :] = (
                    middle[:, at(half + half * part + STEP * k), :] * got[k])
            for side in (odd, 1 - odd):
                @pl.when(jnp.logical_and(m < views // 2 - 1, inside(side)))
                def _(side=side, part=part):
                    rim(m + 1, side, part).start()
        return carry

    lax.fori_loop(0, views // 2, pair, 0)
    result = pltpu.make_async_copy(ext.at[views // 2, :, pl.ds(rows, rows), :], out, load_sem.at[1])
    result.start()

    def drain(m, carry):
        for side in (0, 1):
            @pl.when(inside(side))
            def _(side=side):
                for k in (0, 1):
                    rim(m, side, k).wait_send()
                    shot_rim(m, k, side).wait_send()

        for second in (0, 1):
            @pl.when(2 * m + second > 0)
            def _(second=second):
                shot(2 * m + second).wait_send()
                taps(2 * m + second).wait_send()

        return carry

    lax.fori_loop(0, views // 2, drain, 0)
    result.wait()


def shards(views, tiles, estimate, images, profiles):
    depth, rows, width = estimate.shape
    far = pl.BlockSpec(memory_space=pltpu.HBM)
    return pl.pallas_call(
        functools.partial(kernel, views, tiles),
        out_shape=jax.ShapeDtypeStruct(estimate.shape, estimate.dtype),
        in_specs=[far, far, far],
        out_specs=far,
        scratch_shapes=[
            pltpu.VMEM((views // 2 + 1, depth, 3 * rows, width), jnp.float32),
            pltpu.VMEM((views, depth, rows + 6 * STEP, width), jnp.float32),
            pltpu.VMEM((2, depth, rows + 6 * STEP, width), jnp.float32),
            pltpu.VMEM((depth, rows + 4 * STEP, width), jnp.float32),
            pltpu.VMEM((views, 3, 1, TAPS), jnp.float32),
            pltpu.VMEM((2, 2, 2 * depth * STEP, depth * WIDE), jnp.bfloat16),
            pltpu.VMEM((2, 2, 2, width, width), jnp.bfloat16),
            pltpu.SemaphoreType.DMA((3,)),
            pltpu.SemaphoreType.DMA((views // 2, 2, 2)),
            pltpu.SemaphoreType.DMA((views // 2, 2, 2)),
            pltpu.SemaphoreType.DMA((views, 3)),
            pltpu.SemaphoreType.DMA((views, 3)),
            pltpu.SemaphoreType.DMA((views,)),
            pltpu.SemaphoreType.DMA((views,)),
        ],
        compiler_params=pltpu.CompilerParams(
            collective_id=0, has_side_effects=True, vmem_limit_bytes=64000000),
    )(estimate, images[0], jnp.transpose(profiles, (1, 0, 2)))


def solution(mesh):
    return jax.shard_map(
        functools.partial(shards, mesh.shape["view"], mesh.shape["tile"]),
        mesh=mesh,
        in_specs=(P("view", "tile", None), P("view", None, "tile", None), P("view", None, None)),
        out_specs=P("view", "tile", None),
        check_vma=False,
    )
```

```python
import functools

import jax
import jax.numpy as jnp
from jax import lax
from jax.experimental import pallas as pl
from jax.experimental.pallas import tpu as pltpu
from jax.sharding import PartitionSpec as P

MESH = pl.DeviceIdType.MESH
TAPS = 15
RADIUS = 7
STEP = 8
WIDE = 3 * STEP
AHEAD = 4


def split(value):
    high = value.astype(jnp.bfloat16)
    low = (value - high.astype(jnp.float32)).astype(jnp.bfloat16)
    return high, low


def dot(a, b):
    return jnp.dot(a, b, preferred_element_type=jnp.float32)


def offsets(depth, width):
    lanes = depth * WIDE
    column = lax.broadcasted_iota(jnp.int32, (depth, lanes), 1)
    plane = (column * 2731) >> 16
    dz = plane - lax.broadcasted_iota(jnp.int32, (depth, lanes), 0)
    column = lax.broadcasted_iota(jnp.int32, (STEP, lanes), 1)
    row = column - ((column * 2731) >> 16) * WIDE
    dx = row - lax.broadcasted_iota(jnp.int32, (STEP, lanes), 0) - STEP
    dy = lax.broadcasted_iota(jnp.int32, (width, width), 0) - lax.broadcasted_iota(
        jnp.int32, (width, width), 1
    )
    return dz, dx, dy


def banded(difference, taps, sign):
    result = jnp.zeros(difference.shape, jnp.float32)
    for k in range(TAPS):
        result = jnp.where(difference == sign * (k - RADIUS), taps[:, k : k + 1], result)
    return result


def matrices(profile, dz, dx, dy, sign):
    gz = banded(dz, profile[0], sign)
    gx = banded(dx, profile[1], sign)
    left = (gz[:, None, :] * gx[None, :, :]).reshape(dz.shape[0] * STEP, dz.shape[1])
    return split(left), split(banded(dy, profile[2], sign))


def correlate(block, left, left_high, right_high, right_low):
    depth, _, width = block.shape
    rows = depth * STEP
    flat = [block[:, i * STEP : i * STEP + WIDE, :].reshape(depth * WIDE, width) for i in (0, 1)]
    high, low = split(jnp.concatenate(flat, axis=1))
    both = dot(left, high)
    mid = both[:rows] + (both[rows:] + dot(left_high, low))
    mid = jnp.concatenate([mid[:, :width], mid[:, width:]], axis=0)
    high, low = split(mid)
    out = dot(high, right_high) + (dot(low, right_high) + dot(high, right_low))
    return [out[i * rows : (i + 1) * rows].reshape(depth, STEP, width) for i in (0, 1)]


def kernel(views, tiles, est, img, prof, out, ext, shots, quot, middle, prof_all, zx, yy,
           load_sem, s_send, s_recv, i_send, i_recv, p_send, p_recv):
    view, tile = lax.axis_index("view"), lax.axis_index("tile")
    depth, rows, width = est.shape
    half = rows // 2
    wide = depth * STEP
    skirt = 3 * STEP

    def around(value, size):
        return lax.rem(value + size, size)

    def inside(side):
        return tile != side * (tiles - 1)

    def at(row, size=STEP):
        return pl.ds(pl.multiple_of(row, STEP), size)

    barrier = pltpu.get_barrier_semaphore()
    for side in (0, 1):
        @pl.when(inside(side))
        def _(side=side):
            pl.semaphore_signal(
                barrier, inc=1, device_id=(view, tile + 2 * side - 1), device_id_type=MESH)

    for dv in range(1, views):
        pl.semaphore_signal(
            barrier, inc=1, device_id=(around(view + dv, views), tile), device_id_type=MESH)

    def block(n):
        to = around(view - n, views)
        return to, pl.ds(pl.multiple_of(to * depth, depth), depth)

    own = [
        pltpu.make_async_copy(prof, prof_all.at[0], load_sem.at[0]),
        pltpu.make_async_copy(est, ext.at[0, :, pl.ds(rows, rows), :], load_sem.at[1]),
        pltpu.make_async_copy(
            img.at[block(0)[1]], shots.at[0, :, pl.ds(skirt, rows), :], load_sem.at[2]),
    ]
    for copy in own:
        copy.start()

    def rim(m, side, part, first=False):
        source = est.at[:, at(half * part, half), :] if first else ext.at[
            m, :, at(rows + half * part, half), :]
        return pltpu.make_async_remote_copy(
            src_ref=source,
            dst_ref=ext.at[m, :, at(2 * rows * (1 - side) + half * part, half), :],
            send_sem=s_send.at[m, side, part], recv_sem=s_recv.at[m, side, part],
            device_id=(view, tile + 2 * side - 1), device_id_type=MESH)

    def shot(n):
        to, planes = block(n)
        return pltpu.make_async_remote_copy(
            src_ref=img.at[planes], dst_ref=shots.at[n, :, pl.ds(skirt, rows), :],
            send_sem=i_send.at[n, 2], recv_sem=i_recv.at[n, 2],
            device_id=(to, tile), device_id_type=MESH)

    def shot_rim(m, second, side, outer=False, first=False):
        n = 2 * m + second
        size = half if outer else STEP
        here = STEP if outer else (rows - STEP) * side
        there = (skirt + rows + STEP) * (1 - side) if outer else (
            (skirt + rows) * (1 - side) + half * side)
        source = img.at[block(0)[1], at(here, size), :] if first else shots.at[
            n, :, at(skirt + here, size), :]
        return pltpu.make_async_remote_copy(
            src_ref=source, dst_ref=shots.at[n, :, at(there, size), :],
            send_sem=i_send.at[n, side + 3 * outer], recv_sem=i_recv.at[n, side + 3 * outer],
            device_id=(view, tile + 2 * side - 1), device_id_type=MESH)

    def taps(n):
        return pltpu.make_async_remote_copy(
            src_ref=prof, dst_ref=prof_all.at[n], send_sem=p_send.at[n], recv_sem=p_recv.at[n],
            device_id=(around(view - n, views), tile), device_id_type=MESH)

    def pass_on(m, second):
        shot(2 * m + second).wait_recv()
        for side in (0, 1):
            @pl.when(inside(side))
            def _(side=side):
                shot_rim(m, second, side).start()
                if not second:
                    shot_rim(m, second, side, True).start()

    dz, dx, dy = offsets(depth, width)
    at_end = (tile == 0).astype(jnp.int32) + (tile == tiles - 1).astype(jnp.int32)
    pl.semaphore_wait(barrier, views + 1 - at_end)

    for side in (0, 1):
        @pl.when(inside(side))
        def _(side=side):
            for part in (side, 1 - side):
                rim(0, side, part, True).start()
            shot_rim(0, 0, side, False, True).start()
            shot_rim(0, 0, side, True, True).start()

    for n in range(1, views):
        taps(n).start()
    for n in range(1, AHEAD):
        shot(n).start()
    for copy in own:
        copy.wait()

    odd = lax.rem(tile, 2)

    def product(window, second, back):
        return correlate(window, zx[second, back], zx[second, back, :wide],
                         yy[second, back, 0], yy[second, back, 1])

    def blurred(m, second, i):
        if second:
            return product(middle[:, at(STEP * (i + 1), rows), :], 1, 0)
        return product(ext[m, :, at(STEP * (i + 3), rows), :], 0, 0)

    def keep(m, second, i, edge, got):
        for k in (0, 1):
            value = shots[2 * m + second, :, at(STEP * (i + k) + skirt), :] / got[k]
            if edge is not None:
                beyond = jnp.logical_or(i + k < 0, i + k >= rows // STEP)
                value = jnp.where(jnp.logical_and(edge, beyond), 0.0, value)
            quot[second, :, at(STEP * (i + k + (1 if second else 3))), :] = value

    def pair(m, carry):
        @pl.when(2 * m + AHEAD < views)
        def _():
            shot(2 * m + AHEAD).start()

        @pl.when(2 * m + AHEAD + 1 < views)
        def _():
            shot(2 * m + AHEAD + 1).start()

        for second in (0, 1):
            n = 2 * m + second
            if second:
                taps(n).wait_recv()
            else:
                @pl.when(m > 0)
                def _():
                    taps(n).wait_recv()
            for which, sign in ((0, 1), (1, -1)):
                left, right = matrices(prof_all[n], dz, dx, dy, sign)
                zx[second, which, :wide] = left[0]
                zx[second, which, wide:] = left[1]
                yy[second, which, 0] = right[0]
                yy[second, which, 1] = right[1]

        @pl.when(m > 0)
        def _():
            pass_on(m, 0)

        keep(m, 0, 1, None, blurred(m, 0, 1))
        pass_on(m, 1)

        def arrive(side, copies):
            @pl.when(tile != side * (tiles - 1))
            def _():
                for copy in copies:
                    copy.wait_recv()

        def clear(side):
            @pl.when(tile == side * (tiles - 1))
            def _():
                ext[m, :, at(2 * rows * side, rows), :] = jnp.zeros((depth, rows, width), jnp.float32)

        def first_slab(i):
            got = product(quot[0, :, at(STEP * (i + 2), rows), :], 0, 1)
            for k in (0, 1):
                middle[:, at(STEP * (i + k + 2)), :] = ext[m, :, at(STEP * (i + k + 4)), :] * got[k]

        def second_slab(part):
            got = product(quot[1, :, at(half * part, rows), :], 1, 1)
            for k in (0, 1):
                ext[m + 1, :, at(rows + half * part + STEP * k), :] = (
                    middle[:, at(half + half * part + STEP * k), :] * got[k])
            for side in (odd, 1 - odd):
                @pl.when(jnp.logical_and(m < views // 2 - 1, inside(side)))
                def _(side=side):
                    rim(m + 1, side, part).start()

        for side, waves in ((1 - odd, False), (odd, True)):
            edge = tile == side * (tiles - 1)
            clear(side)
            arrive(side, [rim(m, 1 - side, 1 - side)])
            got = blurred(m, 0, 4 * side - 1)
            arrive(side, [shot_rim(m, 0, 1 - side)])
            keep(m, 0, 4 * side - 1, edge, got)
            first_slab(2 * side)
            if waves:
                keep(m, 1, 1, None, blurred(m, 1, 1))
                second_slab(1 - side)
            arrive(side, [rim(m, 1 - side, side)])
            got = blurred(m, 0, 8 * side - 3)
            arrive(side, [shot_rim(m, 0, 1 - side, True)])
            keep(m, 0, 8 * side - 3, edge, got)
            first_slab(6 * side - 2)
            arrive(side, [shot_rim(m, 1, 1 - side)])
            keep(m, 1, 4 * side - 1, edge, blurred(m, 1, 4 * side - 1))
            if waves:
                second_slab(side)
        return carry

    lax.fori_loop(0, views // 2, pair, 0)
    result = pltpu.make_async_copy(ext.at[views // 2, :, pl.ds(rows, rows), :], out, load_sem.at[1])
    result.start()

    def drain(m, carry):
        for side in (0, 1):
            @pl.when(inside(side))
            def _(side=side):
                for k in (0, 1):
                    rim(m, side, k).wait_send()
                    shot_rim(m, k, side).wait_send()
                shot_rim(m, 0, side, True).wait_send()

        for second in (0, 1):
            @pl.when(2 * m + second > 0)
            def _(second=second):
                shot(2 * m + second).wait_send()
                taps(2 * m + second).wait_send()

        return carry

    lax.fori_loop(0, views // 2, drain, 0)
    result.wait()


def shards(views, tiles, estimate, images, profiles):
    depth, rows, width = estimate.shape
    far = pl.BlockSpec(memory_space=pltpu.HBM)
    return pl.pallas_call(
        functools.partial(kernel, views, tiles),
        out_shape=jax.ShapeDtypeStruct(estimate.shape, estimate.dtype),
        in_specs=[far, far, far],
        out_specs=far,
        scratch_shapes=[
            pltpu.VMEM((views // 2 + 1, depth, 3 * rows, width), jnp.float32),
            pltpu.VMEM((views, depth, rows + 6 * STEP, width), jnp.float32),
            pltpu.VMEM((2, depth, rows + 6 * STEP, width), jnp.float32),
            pltpu.VMEM((depth, rows + 4 * STEP, width), jnp.float32),
            pltpu.VMEM((views, 3, 1, TAPS), jnp.float32),
            pltpu.VMEM((2, 2, 2 * depth * STEP, depth * WIDE), jnp.bfloat16),
            pltpu.VMEM((2, 2, 2, width, width), jnp.bfloat16),
            pltpu.SemaphoreType.DMA((3,)),
            pltpu.SemaphoreType.DMA((views // 2, 2, 2)),
            pltpu.SemaphoreType.DMA((views // 2, 2, 2)),
            pltpu.SemaphoreType.DMA((views, 5)),
            pltpu.SemaphoreType.DMA((views, 5)),
            pltpu.SemaphoreType.DMA((views,)),
            pltpu.SemaphoreType.DMA((views,)),
        ],
        compiler_params=pltpu.CompilerParams(
            collective_id=0, has_side_effects=True, vmem_limit_bytes=64000000),
    )(estimate, images[0], jnp.transpose(profiles, (1, 0, 2)))


def solution(mesh):
    return jax.shard_map(
        functools.partial(shards, mesh.shape["view"], mesh.shape["tile"]),
        mesh=mesh,
        in_specs=(P("view", "tile", None), P("view", None, "tile", None), P("view", None, None)),
        out_specs=P("view", "tile", None),
        check_vma=False,
    )
```
